256 devices in a mesh: row: 8 (over z_hi, core), col: 32 (over y, x, z_lo).
Axes of the slice: x: 4, y: 4, z: 8 (z_hi: 4, z_lo: 2; z = z_hi * 2 + z_lo), core: 2. Of those that a mesh axis runs over, the one named last changes fastest.
Arguments:
- tile_amps: bfloat16 [6144, 6144], P('row', 'col'), as said below
- cycle_ints: bfloat16 [6144, 6144], P('row', 'col'), as said below
- base_ints: bfloat16 [6144, 6144], P('row', 'col'), as said below
- amp_mask: int32 [96, 96], P('row', 'col'), may hold values from 0 to 1, as said below
- int_mask: int32 [96, 96], P('row', 'col'), may hold values from 0 to 1, as said below
- pair_amps: bfloat16 [64, 196608], P(None, ('row', 'col')), may hold values from -6 to 6
- ladder_ints: bfloat16 [196608, 1024], P(('row', 'col')), may hold values from -0.0546875 to 0.0546875
- pair_list: int32 [16], replicated, may hold values from 0 to 63, as said below
Outputs:
- cycle_residual: float32 [6144, 6144], P('row', 'col')
- ladder: float32 [16, 1024], P(None, 'col')
The draws below stay inside these ranges and needn't reach their ends.
Inputs may be any that keep to these rules, and one draw needn't show every extreme that they name: `tile_amps`: equal to its transpose. `cycle_ints`: equal to its transpose. `base_ints`: equal to its transpose. `amp_mask`: 0 or 1, equal to its transpose, 1 on every diagonal tile. `int_mask`: 0 or 1, equal to its transpose, 1 on every diagonal tile. `pair_list`: distinct entries.
All inputs are finite; a program needn't handle non-finite values.
Results may differ from the reference program's by a relative error of at most 0.0029.
Values may be sent and summed in bfloat16 or wider, within the bound.
No kernel may reach another device: no remote copies, remote signals or barrier semaphores. Data moves between devices by JAX's collectives and lax.ppermute only.
A program may use at most 64 MiB of HBM per device.

```python
import jax
import jax.numpy as jnp

TILE = 64
AB = 1024
NPAIRS = 64
PAIRS = 16
N = 6144
NT = 96
CD = 196608


def symmetric_mask(key):
    values = jax.random.randint(key, (NT, NT), 0, 100)
    tile_rows = jnp.arange(NT)[:, None]
    tile_cols = jnp.arange(NT)[None, :]
    mirrored = jnp.where(tile_rows <= tile_cols, values, values.T)
    distance = jnp.abs(tile_rows - tile_cols)
    band_width = max(NT // 4, 1)
    threshold = jnp.maximum(10, 85 - 75 * distance // band_width)
    return jnp.where(distance == 0, 1, (mirrored < threshold).astype(jnp.int32)).astype(jnp.int32)


def draw_amp_mask(key, part):
    return symmetric_mask(jax.random.fold_in(key, 11))


def draw_int_mask(key, part):
    return symmetric_mask(jax.random.fold_in(key, 12))


def normal_field(key):
    entries = jax.random.normal(key, (N, N), jnp.float32)
    return (entries + entries.T) * 0.7071


def draw_tile_amps(key, part):
    inner = jax.random.fold_in(key, 21)
    field = normal_field(inner)
    return (field * N ** (-0.5)).astype(jnp.bfloat16)


def draw_cycle_ints(key, part):
    inner = jax.random.fold_in(key, 22)
    field = normal_field(inner)
    return field.astype(jnp.bfloat16)


def draw_base_ints(key, part):
    inner = jax.random.fold_in(key, 23)
    field = normal_field(inner)
    return field.astype(jnp.bfloat16)


def draw_pair_list(key, part):
    first, second = jax.random.split(jax.random.fold_in(key, 31))
    others = jax.random.permutation(first, NPAIRS - 1)[:PAIRS - 1]
    listed = jnp.concatenate([others, jnp.array([NPAIRS - 1])])
    return jax.random.permutation(second, listed).astype(jnp.int32)


def raised(values, own_key, source, target, parts, factor):
    def block_of(axis_at):
        return (jnp.arange(values.shape[axis_at]) // (values.shape[axis_at] // parts)).reshape((-1,) + (1,) * (values.ndim - 1 - axis_at))

    near = jax.random.permutation(own_key, parts)[block_of(target)]
    second = (block_of(target) + parts // 2) % parts
    return jnp.where((block_of(source) == near) | (block_of(source) == second), factor * values, values)


def block_levels(rng, extent, pieces, low, high):
    gain, own = 1.0, jax.random.fold_in(rng, 6)
    for dim, shards_of in pieces:
        draws = jnp.exp(jax.random.uniform(jax.random.fold_in(own, dim), (shards_of,), jnp.float32, low / len(pieces), high / len(pieces)))
        gain = gain * jnp.repeat(draws, extent[dim] // shards_of).reshape([-1 if axis == dim else 1 for axis in range(len(extent))])
    return gain


def scatter_about(rng, shape, scale, most, cuts=(), held_as=jnp.bfloat16):
    drawn = jax.random.normal(rng, shape, jnp.float32) * scale
    if len(cuts) > 0:
        drawn = block_levels(rng, shape, cuts, -0.22, 0.18) * drawn
    return jnp.clip(drawn, min=-most, max=most).astype(held_as)


def noise_with(key, extent, deviation, limit, cuts, heavy, kind=jnp.bfloat16):
    values = deviation * jax.random.normal(key, extent, jnp.float32)
    if cuts:
        values = values * block_levels(key, extent, cuts, -0.22, 0.18)
    return jnp.clip(raised(values, jax.random.fold_in(key, 3), *heavy), -limit, limit).astype(kind)


def setup_inputs(seed: int = 0) -> dict:
    keys = jax.random.split(jax.random.key(seed), 9)
    return {
        "tile_amps": draw_tile_amps(jax.random.fold_in(keys[8], 71), 0),
        "cycle_ints": draw_cycle_ints(jax.random.fold_in(keys[8], 71), 0),
        "base_ints": draw_base_ints(jax.random.fold_in(keys[8], 71), 0),
        "amp_mask": draw_amp_mask(jax.random.fold_in(keys[8], 71), 0),
        "int_mask": draw_int_mask(jax.random.fold_in(keys[8], 71), 0),
        "pair_amps": scatter_about(keys[5], (NPAIRS, CD), 1.0, 6.0, ((1, 256),)),
        "ladder_ints": noise_with(keys[6], (CD, AB), CD ** -0.5, 0.0546875, ((0, 256),), (0, 1, 256, 6.0)),
        "pair_list": draw_pair_list(jax.random.fold_in(keys[8], 71), 0),
    }


def expand(mask, dtype):
    return jnp.repeat(jnp.repeat(mask, TILE, axis=0), TILE, axis=1).astype(dtype)


def reference(tile_amps, cycle_ints, base_ints, amp_mask, int_mask, pair_amps, ladder_ints, pair_list):
    amplitudes = tile_amps * expand(amp_mask, tile_amps.dtype)
    integrals = cycle_ints * expand(int_mask, cycle_ints.dtype)
    baseline = base_ints * expand(int_mask, base_ints.dtype)
    product = jnp.dot(integrals, amplitudes, preferred_element_type=jnp.float32)
    intermediate = (baseline.astype(jnp.float32) + product).astype(tile_amps.dtype)
    cycle_residual = jnp.dot(amplitudes, intermediate, preferred_element_type=jnp.float32)
    chosen = jnp.take(pair_amps, pair_list.astype(jnp.int32), axis=0)
    ladder = jnp.dot(chosen, ladder_ints, preferred_element_type=jnp.float32)
    return cycle_residual, ladder
```

```python
import functools

import jax
import jax.numpy as jnp
from jax import lax
from jax.experimental import pallas as pl
from jax.experimental.pallas import tpu as pltpu
from jax.sharding import PartitionSpec as P


TILE = 64
F32, BF16 = jnp.float32, jnp.bfloat16
STEPS = (0, -1, 1, 2)


def shift(value, zh=0, core=0, y=0, x=0, zl=0):
    pairs = []
    for r in range(8):
        for c in range(32):
            to_r = ((r // 2 + zh) % 4) * 2 + (r + core) % 2
            to_c = ((c // 8 + y) % 4) * 8 + ((c // 2 + x) % 4) * 2 + (c + zl) % 2
            pairs.append((r * 32 + c, to_r * 32 + to_c))
    return lax.ppermute(value, ("row", "col"), pairs)


def ring(value, axis):
    return [value] + [shift(value, **{axis: -step}) for step in STEPS[1:]]


def place():
    r, c = lax.axis_index("row"), lax.axis_index("col")
    return r // 2, r % 2, c // 8, (c // 2) % 4, c % 2


def swap_middle(t):
    low = lax.broadcasted_iota(jnp.int32, t[0].shape, 1) < TILE
    r = [pltpu.roll(v, TILE, 1) if i in (1, 2, 3, 4) else v for i, v in enumerate(t)]
    return [
        t[0],
        jnp.where(low, t[1], r[3]),
        jnp.where(low, r[3], r[4]),
        jnp.where(low, r[1], r[2]),
        jnp.where(low, r[2], t[4]),
        t[5],
    ]


def prepare_kernel(v_ref, a_ref, b_ref, im_ref, am_ref, va1, va2, b_out, keep, send_a, send_b):
    low = lax.broadcasted_iota(jnp.int32, (TILE, 128), 1) < TILE
    zl = lax.axis_index("col") % 2
    for which, (ref, mask) in enumerate(((v_ref, im_ref), (a_ref, am_ref), (b_ref, im_ref))):
        for k in range(3):
            tiles = []
            for t in range(6):
                block = ref[k * 64 : k * 64 + 64, t * 128 : t * 128 + 128].astype(F32)
                m = jnp.where(low, mask[k, 2 * t], mask[k, 2 * t + 1]).astype(F32)
                tiles.append(block * m)
            tiles = [v.astype(BF16) for v in swap_middle(tiles)]
            rows = slice(k * 64, k * 64 + 64)
            halves = (tiles[0:3], tiles[3:6])
            if which == 0:
                halves = [
                    [jnp.where(zl == 0, p, q) for p, q in zip(*pair)]
                    for pair in ((halves[1], halves[0]), (halves[0], halves[1]))
                ]
            for at, half in enumerate(halves):
                if which == 2:
                    continue
                for t, v in enumerate(half):
                    lanes = slice(t * 128, t * 128 + 128)
                    if k == 0:
                        va1[2 * which + at, 0:64, lanes] = v
                    elif k == 1:
                        va1[2 * which + at, 64:96, lanes] = v[0:32]
                        va2[2 * which + at, 0:32, lanes] = v[32:64]
                    else:
                        va2[2 * which + at, 32:96, lanes] = v
            if which > 0:
                into = keep if which == 1 else b_out
                for t in range(3):
                    lanes = slice(t * 128, t * 128 + 128)
                    into[rows, lanes] = jnp.where(zl == 0, tiles[t], tiles[t + 3])
                    (send_a if which == 1 else send_b)[rows, lanes] = jnp.where(zl == 0, tiles[t + 3], tiles[t])


VMEM = pl.BlockSpec(memory_space=pltpu.VMEM)
SMEM = pl.BlockSpec(memory_space=pltpu.SMEM)
ANY = pl.BlockSpec(memory_space=pl.ANY)


def prepare(vt, at, bt, int_mask, amp_mask):
    struct = jax.ShapeDtypeStruct
    return pl.pallas_call(
        prepare_kernel,
        name="prepare",
        out_shape=(
            struct((4, 96, 384), BF16),
            struct((4, 96, 384), BF16),
            struct((192, 384), BF16),
            struct((192, 384), BF16),
            struct((192, 384), BF16),
            struct((192, 384), BF16),
        ),
        in_specs=[VMEM, VMEM, VMEM, SMEM, SMEM],
        out_specs=(VMEM,) * 6,
        cost_estimate=pl.CostEstimate(flops=10**6, bytes_accessed=2 * 10**6, transcendentals=0),
    )(vt, at, bt, int_mask, amp_mask)


def stack_kernel(a, b, c, d, ints, amps, sem):
    copies = []
    for i, ref in enumerate((a, b, c, d)):
        for part in range(4):
            into = (ints, amps)[part // 2].at[i, part % 2]
            for lane in (0, 128, 256):
                lanes = pl.ds(lane, 128)
                copies.append(
                    pltpu.make_async_copy(ref.at[part, :, lanes], into.at[:, lanes], sem)
                )
    for copy in copies:
        copy.start()
    for copy in copies:
        copy.wait()


def stack(blocks):
    struct = jax.ShapeDtypeStruct
    return pl.pallas_call(
        stack_kernel,
        name="stack",
        out_shape=(struct((4, 2, 96, 384), BF16), struct((4, 2, 96, 384), BF16)),
        in_specs=[ANY] * 4,
        out_specs=(VMEM,) * 2,
        scratch_shapes=[pltpu.SemaphoreType.DMA],
        compiler_params=pltpu.CompilerParams(vmem_limit_bytes=4 << 20),
        cost_estimate=pl.CostEstimate(flops=1000, bytes_accessed=2 * 10**6, transcendentals=0),
    )(*blocks)


def product_kernel(stage, sending, *refs):
    stacks, pieces, (out, w, g, total, w_sems, g_sems) = refs[:8], refs[8:16], refs[16:]
    zh, core, y, x, _ = place()
    rows = slice(None) if stage == 1 else slice(192, 384) if sending else slice(0, 192)
    sides = ((0 if sending else 1),) if stage == 1 else (0, 1)

    @pl.loop(0, 4)
    def _(inner):
        di = jnp.where(inner < 2, 3 * inner, inner - 1)
        for outer, ds in enumerate(STEPS):
            for half in range(2):
                dy, dx = (ds, di) if half == 0 else (di, ds)
                at_y, at_x = lax.rem(y + dy + 4, 4), lax.rem(x + dx + 4, 4)
                row = pl.multiple_of((at_y * 4 + at_x) * 192 + half * 96, 32)
                for at, side in enumerate(sides):
                    for lane in (0, 128, 256):
                        pltpu.make_async_copy(
                            stacks[4 * half + outer].at[inner, side, :, pl.ds(lane, 128)],
                            w.at[pl.ds(row, 96), pl.ds(at * 384 + lane, 128)],
                            w_sems.at[at_y],
                        ).start()

    for i, dz in enumerate(STEPS):
        for other in range(2):
            at_z, at_core = lax.rem(zh + dz + 4, 4), lax.rem(core + other, 2)
            pltpu.make_async_copy(
                pieces[other * 4 + i].at[rows if stage == 2 else slice(0, 384)],
                g.at[at_z, :, pl.ds(pl.multiple_of(at_core * 384, 128), 384)],
                g_sems.at[at_z],
            ).start()
    total[...] = jnp.zeros_like(total)

    @pl.loop(0, 4)
    def _(k):
        part = pl.ds(pl.multiple_of(k * 768, 768), 768)
        pltpu.make_async_copy(w.at[part, :], w.at[part, :], w_sems.at[k]).wait()
        pltpu.make_async_copy(g.at[k], g.at[k], g_sems.at[k]).wait()
        total[...] += jnp.dot(g[k], w[part, :], preferred_element_type=F32)

    if stage == 2:
        for k in range(3):
            part = slice(k * 64, k * 64 + 64)
            tiles = swap_middle([total[part, t * 128 : t * 128 + 128] for t in range(6)])
            for t, v in enumerate(tiles):
                out[part, t * 128 : t * 128 + 128] = v.astype(out.dtype)
    elif sending:
        out[0:192, :] = total[192:384].astype(BF16)
        out[192:384, :] = total[0:192].astype(BF16)
    else:
        out[...] = total[...]


def product(stage, sending, stacks, pieces):
    rows, width = (384, 384) if stage == 1 else (192, 768)
    return pl.pallas_call(
        functools.partial(product_kernel, stage, sending),
        out_shape=jax.ShapeDtypeStruct((rows, width), BF16 if sending else F32),
        in_specs=[ANY] * 16,
        out_specs=VMEM,
        scratch_shapes=[
            pltpu.VMEM((3072, width), BF16),
            pltpu.VMEM((4, rows, 768), BF16),
            pltpu.VMEM((rows, width), F32),
            pltpu.SemaphoreType.DMA((4,)),
            pltpu.SemaphoreType.DMA((4,)),
        ],
        compiler_params=pltpu.CompilerParams(vmem_limit_bytes=16 << 20),
        cost_estimate=pl.CostEstimate(
            flops=384 * 768 * 3072, bytes_accessed=5 * 10**6, transcendentals=0
        ),
    )(*stacks, *pieces)


def right_operand(piece):
    mine = ring(piece, "zh")
    return mine + [shift(v, core=1) for v in mine]


def ladder_kernel(pair_list, pair_amps, ladder_ints, out):
    row = lax.broadcasted_iota(jnp.int32, (16, 64), 0)
    column = lax.broadcasted_iota(jnp.int32, (16, 64), 1)
    wanted = jnp.zeros((16, 64), jnp.int32)
    for i in range(16):
        wanted = jnp.where(row == i, pair_list[i], wanted)
    selector = jnp.where(wanted == column, 1.0, 0.0).astype(BF16)
    chosen = jnp.dot(selector, pair_amps[...], preferred_element_type=F32).astype(BF16)
    sums = jnp.dot(chosen, ladder_ints[...], preferred_element_type=F32)
    for c in range(32):
        out[c] = sums[:, c * 32 : c * 32 + 32]


def ladder_part(pair_amps, ladder_ints, pair_list):
    return pl.pallas_call(
        ladder_kernel,
        name="ladder",
        out_shape=jax.ShapeDtypeStruct((32, 16, 32), F32),
        in_specs=[SMEM, VMEM, VMEM],
        out_specs=VMEM,
        cost_estimate=pl.CostEstimate(
            flops=25 * 10**6, bytes_accessed=2 * 10**6, transcendentals=0
        ),
    )(pair_list, pair_amps, ladder_ints)


def on_device(
    tile_amps, cycle_ints, base_ints, amp_mask, int_mask, pair_amps, ladder_ints, pair_list
):
    va1, va2, base, keep, send_a, send_b = prepare(
        cycle_ints.T, tile_amps.T, base_ints.T, int_mask.T, amp_mask.T
    )
    came = shift(send_a, zl=1)
    x_blocks, y_blocks = ring(va1, "x"), ring(va2, "y")
    right = right_operand(jnp.concatenate([keep, came], axis=0))
    ints1, amps1 = stack(x_blocks)
    ints2, amps2 = stack(y_blocks)
    stacks = ring(ints1, "y") + ring(ints2, "x")
    send = product(1, True, stacks, right)
    came = shift(send, zl=1)
    keep = product(1, False, stacks, right)
    base = jnp.concatenate([base, shift(send_b, zl=1)], axis=0)

    parts = ladder_part(pair_amps, ladder_ints, pair_list)
    mine = lax.all_to_all(parts, "col", 0, 0)
    mine = mine.sum(axis=0)
    high = lax.reduce_precision(mine, 8, 7)
    rows = jnp.concatenate([high, mine - high], axis=1).astype(BF16)
    rows = jnp.pad(rows, ((0, 0), (0, 320)))

    stacks = ring(amps1, "y") + ring(amps2, "x")
    piece = base.astype(F32) + (keep + came.astype(F32))
    right = right_operand(jnp.concatenate([piece.astype(BF16), rows], axis=0))
    send = product(2, True, stacks, right)
    came = shift(send, zl=1)
    mine = [v[384:400, 0:64].astype(F32) for v in right]
    mine = functools.reduce(jnp.add, mine)
    ladder = mine[:, 0:32] + mine[:, 32:64]
    keep = product(2, False, stacks, right)
    return (keep + came.astype(F32)).T, ladder


def solution(mesh):
    in_specs = (
        P("row", "col"),
        P("row", "col"),
        P("row", "col"),
        P("row", "col"),
        P("row", "col"),
        P(None, ("row", "col")),
        P(("row", "col"), None),
        P(),
    )
    out_specs = (P("row", "col"), P(None, "col"))
    return jax.shard_map(
        on_device, mesh=mesh, in_specs=in_specs, out_specs=out_specs, check_vma=False
    )
```

```python
import functools

import jax
import jax.numpy as jnp
from jax import lax
from jax.experimental import pallas as pl
from jax.experimental.pallas import tpu as pltpu
from jax.sharding import PartitionSpec as P


TILE = 64
F32, BF16 = jnp.float32, jnp.bfloat16
STEPS = (0, -1, 1, 2)


def shift(value, zh=0, core=0, y=0, x=0, zl=0):
    pairs = []
    for r in range(8):
        for c in range(32):
            to_r = ((r // 2 + zh) % 4) * 2 + (r + core) % 2
            to_c = ((c // 8 + y) % 4) * 8 + ((c // 2 + x) % 4) * 2 + (c + zl) % 2
            pairs.append((r * 32 + c, to_r * 32 + to_c))
    return lax.ppermute(value, ("row", "col"), pairs)


def ring(value, axis):
    return [value] + [shift(value, **{axis: -step}) for step in STEPS[1:]]


def place():
    r, c = lax.axis_index("row"), lax.axis_index("col")
    return r // 2, r % 2, c // 8, (c // 2) % 4, c % 2


def swap_middle(t):
    low = lax.broadcasted_iota(jnp.int32, t[0].shape, 1) < TILE
    r = [pltpu.roll(v, TILE, 1) if i in (1, 2, 3, 4) else v for i, v in enumerate(t)]
    return [
        t[0],
        jnp.where(low, t[1], r[3]),
        jnp.where(low, r[3], r[4]),
        jnp.where(low, r[1], r[2]),
        jnp.where(low, r[2], t[4]),
        t[5],
    ]


def prepare_kernel(v_ref, a_ref, b_ref, im_ref, am_ref, va1, va2, b_out, keep, send_a, send_b):
    low = lax.broadcasted_iota(jnp.int32, (TILE, 128), 1) < TILE
    zl = lax.axis_index("col") % 2
    for which, (ref, mask) in enumerate(((v_ref, im_ref), (a_ref, am_ref), (b_ref, im_ref))):
        for k in range(3):
            tiles = []
            for t in range(6):
                block = ref[k * 64 : k * 64 + 64, t * 128 : t * 128 + 128].astype(F32)
                m = jnp.where(low, mask[k, 2 * t], mask[k, 2 * t + 1]).astype(F32)
                tiles.append(block * m)
            tiles = [v.astype(BF16) for v in swap_middle(tiles)]
            rows = slice(k * 64, k * 64 + 64)
            halves = (tiles[0:3], tiles[3:6])
            if which == 0:
                halves = [
                    [jnp.where(zl == 0, p, q) for p, q in zip(*pair)]
                    for pair in ((halves[1], halves[0]), (halves[0], halves[1]))
                ]
            for at, half in enumerate(halves):
                if which == 2:
                    continue
                for t, v in enumerate(half):
                    lanes = slice(t * 128, t * 128 + 128)
                    if k == 0:
                        va1[2 * which + at, 0:64, lanes] = v
                    elif k == 1:
                        va1[2 * which + at, 64:96, lanes] = v[0:32]
                        va2[2 * which + at, 0:32, lanes] = v[32:64]
                    else:
                        va2[2 * which + at, 32:96, lanes] = v
            if which > 0:
                into = keep if which == 1 else b_out
                for t in range(3):
                    lanes = slice(t * 128, t * 128 + 128)
                    into[rows, lanes] = jnp.where(zl == 0, tiles[t], tiles[t + 3])
                    (send_a if which == 1 else send_b)[rows, lanes] = jnp.where(zl == 0, tiles[t + 3], tiles[t])


VMEM = pl.BlockSpec(memory_space=pltpu.VMEM)
SMEM = pl.BlockSpec(memory_space=pltpu.SMEM)
ANY = pl.BlockSpec(memory_space=pl.ANY)


def prepare(vt, at, bt, int_mask, amp_mask):
    struct = jax.ShapeDtypeStruct
    return pl.pallas_call(
        prepare_kernel,
        name="prepare",
        compiler_params=pltpu.CompilerParams(vmem_limit_bytes=65600000),
        out_shape=(
            struct((4, 96, 384), BF16),
            struct((4, 96, 384), BF16),
            struct((192, 384), BF16),
            struct((192, 384), BF16),
            struct((192, 384), BF16),
            struct((192, 384), BF16),
        ),
        in_specs=[VMEM, VMEM, VMEM, SMEM, SMEM],
        out_specs=(VMEM,) * 6,
        cost_estimate=pl.CostEstimate(flops=10**6, bytes_accessed=2 * 10**6, transcendentals=0),
    )(vt, at, bt, int_mask, amp_mask)


def join_kernel(a, b, out, sem):
    copies = []
    for i, ref in enumerate((a, b)):
        for lane in (0, 128, 256):
            lanes = pl.ds(lane, 128)
            into = out.at[pl.ds(192 * i, 192), lanes]
            copies.append(pltpu.make_async_copy(ref.at[:, lanes], into, sem))
    for copy in copies:
        copy.start()
    for copy in copies:
        copy.wait()


def join(a, b):
    return pl.pallas_call(
        join_kernel,
        name="join",
        out_shape=jax.ShapeDtypeStruct((384, 384), BF16),
        in_specs=[ANY] * 2,
        out_specs=VMEM,
        scratch_shapes=[pltpu.SemaphoreType.DMA],
        compiler_params=pltpu.CompilerParams(vmem_limit_bytes=4 << 20),
        cost_estimate=pl.CostEstimate(flops=1000, bytes_accessed=6 * 10**5, transcendentals=0),
    )(a, b)


def stack_kernel(a, b, c, d, ints, amps, sem):
    copies = []
    for i, ref in enumerate((a, b, c, d)):
        for part in range(4):
            into = (ints, amps)[part // 2].at[i, part % 2]
            for lane in (0, 128, 256):
                lanes = pl.ds(lane, 128)
                copies.append(
                    pltpu.make_async_copy(ref.at[part, :, lanes], into.at[:, lanes], sem)
                )
    for copy in copies:
        copy.start()
    for copy in copies:
        copy.wait()


def stack(blocks):
    struct = jax.ShapeDtypeStruct
    return pl.pallas_call(
        stack_kernel,
        name="stack",
        out_shape=(struct((4, 2, 96, 384), BF16), struct((4, 2, 96, 384), BF16)),
        in_specs=[ANY] * 4,
        out_specs=(VMEM,) * 2,
        scratch_shapes=[pltpu.SemaphoreType.DMA],
        compiler_params=pltpu.CompilerParams(vmem_limit_bytes=4 << 20),
        cost_estimate=pl.CostEstimate(flops=1000, bytes_accessed=2 * 10**6, transcendentals=0),
    )(*blocks)


def product_kernel(stage, sending, *refs):
    stacks, pieces, (out, w, g, total, w_sems, g_sems) = refs[:8], refs[8:16], refs[16:]
    zh, core, y, x, _ = place()
    count = g.shape[1]
    sides = ((0 if sending else 1),) if stage == 1 else (0, 1)

    @pl.loop(0, 4)
    def _(inner):
        di = jnp.where(inner < 2, 3 * inner, inner - 1)
        for outer, ds in enumerate(STEPS):
            for half in range(2):
                dy, dx = (ds, di) if half == 0 else (di, ds)
                at_y, at_x = lax.rem(y + dy + 4, 4), lax.rem(x + dx + 4, 4)
                row = pl.multiple_of((at_y * 4 + at_x) * 192 + half * 96, 32)
                for at, side in enumerate(sides):
                    for lane in (0, 128, 256):
                        pltpu.make_async_copy(
                            stacks[4 * half + outer].at[inner, side, :, pl.ds(lane, 128)],
                            w.at[pl.ds(row, 96), pl.ds(at * 384 + lane, 128)],
                            w_sems.at[at_y],
                        ).start()

    for i, dz in enumerate(STEPS):
        for other in range(2):
            at_z, at_core = lax.rem(zh + dz + 4, 4), lax.rem(core + other, 2)
            pltpu.make_async_copy(
                pieces[other * 4 + i].at[pl.ds(0, count)],
                g.at[at_z, :, pl.ds(pl.multiple_of(at_core * 384, 128), 384)],
                g_sems.at[at_z],
            ).start()
    total[...] = jnp.zeros_like(total)

    @pl.loop(0, 4)
    def _(k):
        part = pl.ds(pl.multiple_of(k * 768, 768), 768)
        pltpu.make_async_copy(w.at[part, :], w.at[part, :], w_sems.at[k]).wait()
        pltpu.make_async_copy(g.at[k], g.at[k], g_sems.at[k]).wait()
        total[...] += jnp.dot(g[k], w[part, :], preferred_element_type=F32)

    if stage == 2:
        for k in range(3):
            part = slice(k * 64, k * 64 + 64)
            tiles = swap_middle([total[part, t * 128 : t * 128 + 128] for t in range(6)])
            for t, v in enumerate(tiles):
                out[part, t * 128 : t * 128 + 128] = v.astype(out.dtype)
    elif sending:
        out[0:192, :] = total[192:384].astype(BF16)
        out[192:384, :] = total[0:192].astype(BF16)
    else:
        out[...] = total[...]


def product(stage, sending, stacks, pieces):
    rows, width = (384, 384) if stage == 1 else (192, 768)
    return pl.pallas_call(
        functools.partial(product_kernel, stage, sending),
        out_shape=jax.ShapeDtypeStruct((rows, width), BF16 if sending else F32),
        in_specs=[ANY] * 16,
        out_specs=VMEM,
        scratch_shapes=[
            pltpu.VMEM((3072, width), BF16),
            pltpu.VMEM((4, rows, 768), BF16),
            pltpu.VMEM((rows, width), F32),
            pltpu.SemaphoreType.DMA((4,)),
            pltpu.SemaphoreType.DMA((4,)),
        ],
        compiler_params=pltpu.CompilerParams(vmem_limit_bytes=16 << 20),
        cost_estimate=pl.CostEstimate(
            flops=384 * 768 * 3072, bytes_accessed=5 * 10**6, transcendentals=0
        ),
    )(*stacks, *pieces)


def right_operand(piece):
    mine = ring(piece, "zh")
    return mine + [shift(v, core=1) for v in mine]


def ladder_kernel(pair_list, pair_amps, ladder_ints, out):
    row = lax.broadcasted_iota(jnp.int32, (16, 64), 0)
    column = lax.broadcasted_iota(jnp.int32, (16, 64), 1)
    wanted = jnp.zeros((16, 64), jnp.int32)
    for i in range(16):
        wanted = jnp.where(row == i, pair_list[i], wanted)
    selector = jnp.where(wanted == column, 1.0, 0.0).astype(BF16)
    chosen = jnp.dot(selector, pair_amps[...], preferred_element_type=F32).astype(BF16)
    sums = jnp.dot(chosen, ladder_ints[...], preferred_element_type=F32)
    for c in range(32):
        for j in range(4):
            out[c, :, j * 32 : j * 32 + 32] = sums[j * 4 : j * 4 + 4, c * 32 : c * 32 + 32]


def ladder_sum_kernel(parts, out):
    total = jnp.concatenate([jnp.sum(parts[...], axis=0), jnp.zeros((12, 128), F32)], axis=0)
    high = total.astype(BF16)
    out[:, 0:128] = high
    out[:, 128:256] = (total - high.astype(F32)).astype(BF16)
    out[:, 256:384] = jnp.zeros((16, 128), BF16)


def ladder_sum(parts):
    return pl.pallas_call(
        ladder_sum_kernel,
        name="ladder_sum",
        compiler_params=pltpu.CompilerParams(vmem_limit_bytes=1 << 20),
        out_shape=jax.ShapeDtypeStruct((16, 384), BF16),
        in_specs=[VMEM],
        out_specs=VMEM,
        cost_estimate=pl.CostEstimate(flops=20000, bytes_accessed=80000, transcendentals=0),
    )(parts)


def ladder_part(pair_amps, ladder_ints, pair_list):
    return pl.pallas_call(
        ladder_kernel,
        name="ladder",
        compiler_params=pltpu.CompilerParams(vmem_limit_bytes=6 << 20),
        out_shape=jax.ShapeDtypeStruct((32, 4, 128), F32),
        in_specs=[SMEM, VMEM, VMEM],
        out_specs=VMEM,
        cost_estimate=pl.CostEstimate(
            flops=25 * 10**6, bytes_accessed=2 * 10**6, transcendentals=0
        ),
    )(pair_list, pair_amps, ladder_ints)


def ladder_end_kernel(*refs):
    pieces, (out, rows, sem) = refs[:8], refs[8:]
    copies = []
    for i, ref in enumerate(pieces):
        copies.append(pltpu.make_async_copy(ref.at[pl.ds(192, 16)], rows.at[i], sem))
    for copy in copies:
        copy.start()
    for copy in copies:
        copy.wait()
    total = rows[0].astype(F32)
    for i in range(1, 8):
        total += rows[i].astype(F32)
    total = total[0:4, 0:128] + total[0:4, 128:256]
    for j in range(4):
        out[j * 4 : j * 4 + 4, :] = total[:, j * 32 : j * 32 + 32]


def ladder_end(pieces):
    return pl.pallas_call(
        ladder_end_kernel,
        name="ladder_end",
        out_shape=jax.ShapeDtypeStruct((16, 32), F32),
        in_specs=[ANY] * 8,
        out_specs=VMEM,
        scratch_shapes=[pltpu.VMEM((8, 16, 384), BF16), pltpu.SemaphoreType.DMA],
        compiler_params=pltpu.CompilerParams(vmem_limit_bytes=1 << 20),
        cost_estimate=pl.CostEstimate(flops=20000, bytes_accessed=100000, transcendentals=0),
    )(*pieces)


def on_device(
    tile_amps, cycle_ints, base_ints, amp_mask, int_mask, pair_amps, ladder_ints, pair_list
):
    va1, va2, base, keep, send_a, send_b = prepare(
        cycle_ints.T, tile_amps.T, base_ints.T, int_mask.T, amp_mask.T
    )
    came = shift(send_a, zl=1)
    x_blocks, y_blocks = ring(va1, "x"), ring(va2, "y")
    right = right_operand(join(keep, came))
    ints1, amps1 = stack(x_blocks)
    ints2, amps2 = stack(y_blocks)
    stacks = ring(ints1, "y") + ring(ints2, "x")
    send = product(1, True, stacks, right)
    came = shift(send, zl=1)
    keep = product(1, False, stacks, right)
    base = jnp.concatenate([base, shift(send_b, zl=1)], axis=0)

    parts = ladder_part(pair_amps, ladder_ints, pair_list)
    parts = lax.all_to_all(parts, "col", 0, 0)
    rows = ladder_sum(parts)

    stacks = ring(amps1, "y") + ring(amps2, "x")
    piece = (base.astype(F32) + (keep + came.astype(F32))).astype(BF16)
    away = right_operand(piece[192:])
    mine = right_operand(jnp.concatenate([piece[:192], rows], axis=0))
    send = product(2, True, stacks, away)
    came = shift(send, zl=1)
    keep = product(2, False, stacks, mine)
    keep, *mine = lax.optimization_barrier((keep, *mine))
    ladder = ladder_end(mine)
    return (keep + came.astype(F32)).T, ladder


def solution(mesh):
    in_specs = (
        P("row", "col"),
        P("row", "col"),
        P("row", "col"),
        P("row", "col"),
        P("row", "col"),
        P(None, ("row", "col")),
        P(("row", "col"), None),
        P(),
    )
    out_specs = (P("row", "col"), P(None, "col"))
    return jax.shard_map(
        on_device, mesh=mesh, in_specs=in_specs, out_specs=out_specs, check_vma=False
    )
```

```python
import functools

import jax
import jax.numpy as jnp
from jax import lax
from jax.experimental import pallas as pl
from jax.experimental.pallas import tpu as pltpu
from jax.sharding import PartitionSpec as P


TILE = 64
F32, BF16 = jnp.float32, jnp.bfloat16
STEPS = (0, -1, 1, 2)


def shift(value, zh=0, core=0, y=0, x=0, zl=0):
    pairs = []
    for r in range(8):
        for c in range(32):
            to_r = ((r // 2 + zh) % 4) * 2 + (r + core) % 2
            to_c = ((c // 8 + y) % 4) * 8 + ((c // 2 + x) % 4) * 2 + (c + zl) % 2
            pairs.append((r * 32 + c, to_r * 32 + to_c))
    return lax.ppermute(value, ("row", "col"), pairs)


def ring(value, axis):
    return [value] + [shift(value, **{axis: -step}) for step in STEPS[1:]]


def place():
    r, c = lax.axis_index("row"), lax.axis_index("col")
    return r // 2, r % 2, c // 8, (c // 2) % 4, c % 2


def swap_middle(t):
    low = lax.broadcasted_iota(jnp.int32, t[0].shape, 1) < TILE
    r = [pltpu.roll(v, TILE, 1) if i in (1, 2, 3, 4) else v for i, v in enumerate(t)]
    return [
        t[0],
        jnp.where(low, t[1], r[3]),
        jnp.where(low, r[3], r[4]),
        jnp.where(low, r[1], r[2]),
        jnp.where(low, r[2], t[4]),
        t[5],
    ]


def prepare_kernel(v_ref, a_ref, b_ref, im_ref, am_ref, va1, va2, b_out, keep, send):
    low = lax.broadcasted_iota(jnp.int32, (TILE, 128), 1) < TILE
    zl = lax.axis_index("col") % 2
    for which, (ref, mask) in enumerate(((v_ref, im_ref), (a_ref, am_ref), (b_ref, im_ref))):
        for k in range(3):
            tiles = []
            for t in range(6):
                block = ref[k * 64 : k * 64 + 64, t * 128 : t * 128 + 128].astype(F32)
                m = jnp.where(low, mask[k, 2 * t], mask[k, 2 * t + 1]).astype(F32)
                tiles.append(block * m)
            tiles = [v.astype(BF16) for v in swap_middle(tiles)]
            rows = slice(k * 64, k * 64 + 64)
            halves = (tiles[0:3], tiles[3:6])
            if which == 0:
                halves = [
                    [jnp.where(zl == 0, p, q) for p, q in zip(*pair)]
                    for pair in ((halves[1], halves[0]), (halves[0], halves[1]))
                ]
            for at, half in enumerate(halves):
                if which == 2:
                    continue
                for t, v in enumerate(half):
                    lanes = slice(t * 128, t * 128 + 128)
                    if k == 0:
                        va1[2 * which + at, 0:64, lanes] = v
                    elif k == 1:
                        va1[2 * which + at, 64:96, lanes] = v[0:32]
                        va2[2 * which + at, 0:32, lanes] = v[32:64]
                    else:
                        va2[2 * which + at, 32:96, lanes] = v
            if which > 0:
                into = keep if which == 1 else b_out
                for t in range(3):
                    lanes = slice(t * 128, t * 128 + 128)
                    into[rows, lanes] = jnp.where(zl == 0, tiles[t], tiles[t + 3])
                    send[which - 1, rows, lanes] = jnp.where(zl == 0, tiles[t + 3], tiles[t])


VMEM = pl.BlockSpec(memory_space=pltpu.VMEM)
SMEM = pl.BlockSpec(memory_space=pltpu.SMEM)
ANY = pl.BlockSpec(memory_space=pl.ANY)


def prepare(vt, at, bt, int_mask, amp_mask):
    struct = jax.ShapeDtypeStruct
    return pl.pallas_call(
        prepare_kernel,
        name="prepare",
        compiler_params=pltpu.CompilerParams(vmem_limit_bytes=65600000),
        out_shape=(
            struct((4, 96, 384), BF16),
            struct((4, 96, 384), BF16),
            struct((192, 384), BF16),
            struct((192, 384), BF16),
            struct((2, 192, 384), BF16),
        ),
        in_specs=[VMEM, VMEM, VMEM, SMEM, SMEM],
        out_specs=(VMEM,) * 5,
        cost_estimate=pl.CostEstimate(flops=10**6, bytes_accessed=2 * 10**6, transcendentals=0),
    )(vt, at, bt, int_mask, amp_mask)


def join_kernel(a, b, out, sem):
    copies = []
    for i, ref in enumerate((a, b.at[0])):
        for lane in (0, 128, 256):
            lanes = pl.ds(lane, 128)
            into = out.at[pl.ds(192 * i, 192), lanes]
            copies.append(pltpu.make_async_copy(ref.at[:, lanes], into, sem))
    for copy in copies:
        copy.start()
    for copy in copies:
        copy.wait()


def join(a, b):
    return pl.pallas_call(
        join_kernel,
        name="join",
        out_shape=jax.ShapeDtypeStruct((384, 384), BF16),
        in_specs=[ANY] * 2,
        out_specs=VMEM,
        scratch_shapes=[pltpu.SemaphoreType.DMA],
        compiler_params=pltpu.CompilerParams(vmem_limit_bytes=4 << 20),
        cost_estimate=pl.CostEstimate(flops=1000, bytes_accessed=6 * 10**5, transcendentals=0),
    )(a, b)


def stack_kernel(a, b, c, d, ints, amps, sem):
    copies = []
    for i, ref in enumerate((a, b, c, d)):
        for part in range(4):
            into = (ints, amps)[part // 2].at[i, part % 2]
            for lane in (0, 128, 256):
                lanes = pl.ds(lane, 128)
                copies.append(
                    pltpu.make_async_copy(ref.at[part, :, lanes], into.at[:, lanes], sem)
                )
    for copy in copies:
        copy.start()
    for copy in copies:
        copy.wait()


def stack(blocks):
    struct = jax.ShapeDtypeStruct
    return pl.pallas_call(
        stack_kernel,
        name="stack",
        out_shape=(struct((4, 2, 96, 384), BF16), struct((4, 2, 96, 384), BF16)),
        in_specs=[ANY] * 4,
        out_specs=(VMEM,) * 2,
        scratch_shapes=[pltpu.SemaphoreType.DMA],
        compiler_params=pltpu.CompilerParams(vmem_limit_bytes=4 << 20),
        cost_estimate=pl.CostEstimate(flops=1000, bytes_accessed=2 * 10**6, transcendentals=0),
    )(*blocks)


def product_kernel(stage, sending, *refs):
    stacks, pieces, (*outs, w, g, total, w_sems, g_sems) = refs[:8], refs[8:16], refs[16:]
    zh, core, y, x, _ = place()
    count = g.shape[1]
    sides = ((0 if sending else 1),) if stage == 1 else (0, 1)

    @pl.loop(0, 4)
    def _(inner):
        di = jnp.where(inner < 2, 3 * inner, inner - 1)
        for outer, ds in enumerate(STEPS):
            for half in range(2):
                dy, dx = (ds, di) if half == 0 else (di, ds)
                at_y, at_x = lax.rem(y + dy + 4, 4), lax.rem(x + dx + 4, 4)
                row = pl.multiple_of((at_y * 4 + at_x) * 192 + half * 96, 32)
                for at, side in enumerate(sides):
                    for lane in (0, 128, 256):
                        pltpu.make_async_copy(
                            stacks[4 * half + outer].at[inner, side, :, pl.ds(lane, 128)],
                            w.at[pl.ds(row, 96), pl.ds(at * 384 + lane, 128)],
                            w_sems.at[at_y],
                        ).start()

    for i, dz in enumerate(STEPS):
        for other in range(2):
            at_z, at_core = lax.rem(zh + dz + 4, 4), lax.rem(core + other, 2)
            pltpu.make_async_copy(
                pieces[other * 4 + i].at[pl.ds(0, count)],
                g.at[at_z, :, pl.ds(pl.multiple_of(at_core * 384, 128), 384)],
                g_sems.at[at_z],
            ).start()
    total[...] = jnp.zeros_like(total)

    @pl.loop(0, 4)
    def _(k):
        part = pl.ds(pl.multiple_of(k * 768, 768), 768)
        pltpu.make_async_copy(w.at[part, :], w.at[part, :], w_sems.at[k]).wait()
        pltpu.make_async_copy(g.at[k], g.at[k], g_sems.at[k]).wait()
        total[...] += jnp.dot(g[k], w[part, :], preferred_element_type=F32)

    if stage == 2:
        (out,) = outs
        for k in range(3):
            part = slice(k * 64, k * 64 + 64)
            tiles = swap_middle([total[part, t * 128 : t * 128 + 128] for t in range(6)])
            for t, v in enumerate(tiles):
                out[part, t * 128 : t * 128 + 128] = v.astype(out.dtype)
    else:
        own, away = total[0:192], total[192:384]
        outs[0][...] = (own if sending else away).astype(outs[0].dtype)
        outs[1][...] = (away if sending else own).astype(outs[1].dtype)


def product(stage, sending, stacks, pieces):
    rows, width = (384, 384) if stage == 1 else (192, 768)
    return pl.pallas_call(
        functools.partial(product_kernel, stage, sending),
        out_shape=(jax.ShapeDtypeStruct((192, width), BF16 if sending else F32),) * (3 - stage),
        in_specs=[ANY] * 16,
        out_specs=(VMEM,) * (3 - stage),
        scratch_shapes=[
            pltpu.VMEM((3072, width), BF16),
            pltpu.VMEM((4, rows, 768), BF16),
            pltpu.VMEM((rows, width), F32),
            pltpu.SemaphoreType.DMA((4,)),
            pltpu.SemaphoreType.DMA((4,)),
        ],
        compiler_params=pltpu.CompilerParams(vmem_limit_bytes=16 << 20),
        cost_estimate=pl.CostEstimate(
            flops=384 * 768 * 3072, bytes_accessed=5 * 10**6, transcendentals=0
        ),
    )(*stacks, *pieces)


def right_operand(piece, via):
    before = shift(piece, zh=1)
    after = shift(piece, zh=-1)
    far = shift(after, zh=-1) if via < 0 else shift(before, zh=1)
    mine = [piece, before, after, far]
    return mine + [shift(v, core=1) for v in mine]


def ladder_kernel(pair_list, pair_amps, ladder_ints, out):
    row = lax.broadcasted_iota(jnp.int32, (16, 64), 0)
    column = lax.broadcasted_iota(jnp.int32, (16, 64), 1)
    wanted = jnp.zeros((16, 64), jnp.int32)
    for i in range(16):
        wanted = jnp.where(row == i, pair_list[i], wanted)
    selector = jnp.where(wanted == column, 1.0, 0.0).astype(BF16)
    chosen = jnp.dot(selector, pair_amps[...], preferred_element_type=F32).astype(BF16)
    sums = jnp.dot(chosen, ladder_ints[...], preferred_element_type=F32)
    for c in range(32):
        for j in range(4):
            out[c, :, j * 32 : j * 32 + 32] = sums[j * 4 : j * 4 + 4, c * 32 : c * 32 + 32]


def ladder_sum_kernel(parts, out):
    total = jnp.concatenate([jnp.sum(parts[...], axis=0), jnp.zeros((12, 128), F32)], axis=0)
    high = total.astype(BF16)
    out[:, 0:128] = high
    out[:, 128:256] = (total - high.astype(F32)).astype(BF16)
    out[:, 256:384] = jnp.zeros((16, 128), BF16)


def ladder_sum(parts):
    return pl.pallas_call(
        ladder_sum_kernel,
        name="ladder_sum",
        compiler_params=pltpu.CompilerParams(vmem_limit_bytes=1 << 20),
        out_shape=jax.ShapeDtypeStruct((16, 384), BF16),
        in_specs=[VMEM],
        out_specs=VMEM,
        cost_estimate=pl.CostEstimate(flops=20000, bytes_accessed=80000, transcendentals=0),
    )(parts)


def ladder_part(pair_amps, ladder_ints, pair_list):
    return pl.pallas_call(
        ladder_kernel,
        name="ladder",
        compiler_params=pltpu.CompilerParams(vmem_limit_bytes=6 << 20),
        out_shape=jax.ShapeDtypeStruct((32, 4, 128), F32),
        in_specs=[SMEM, VMEM, VMEM],
        out_specs=VMEM,
        cost_estimate=pl.CostEstimate(
            flops=25 * 10**6, bytes_accessed=2 * 10**6, transcendentals=0
        ),
    )(pair_list, pair_amps, ladder_ints)


def ladder_end_kernel(*refs):
    pieces, (out, rows, sem) = refs[:8], refs[8:]
    copies = []
    for i, ref in enumerate(pieces):
        copies.append(pltpu.make_async_copy(ref.at[pl.ds(192, 16)], rows.at[i], sem))
    for copy in copies:
        copy.start()
    for copy in copies:
        copy.wait()
    total = rows[0].astype(F32)
    for i in range(1, 8):
        total += rows[i].astype(F32)
    total = total[0:4, 0:128] + total[0:4, 128:256]
    for j in range(4):
        out[j * 4 : j * 4 + 4, :] = total[:, j * 32 : j * 32 + 32]


def ladder_end(pieces):
    return pl.pallas_call(
        ladder_end_kernel,
        name="ladder_end",
        out_shape=jax.ShapeDtypeStruct((16, 32), F32),
        in_specs=[ANY] * 8,
        out_specs=VMEM,
        scratch_shapes=[pltpu.VMEM((8, 16, 384), BF16), pltpu.SemaphoreType.DMA],
        compiler_params=pltpu.CompilerParams(vmem_limit_bytes=1 << 20),
        cost_estimate=pl.CostEstimate(flops=20000, bytes_accessed=100000, transcendentals=0),
    )(*pieces)


def on_device(
    tile_amps, cycle_ints, base_ints, amp_mask, int_mask, pair_amps, ladder_ints, pair_list
):
    va1, va2, base, keep, send = prepare(
        cycle_ints.T, tile_amps.T, base_ints.T, int_mask.T, amp_mask.T
    )
    swapped = shift(send, zl=1)
    x_blocks, y_blocks = ring(va1, "x"), ring(va2, "y")
    right = right_operand(join(keep, swapped), -1)
    ints1, amps1 = stack(x_blocks)
    ints2, amps2 = stack(y_blocks)
    stacks = ring(ints1, "y") + ring(ints2, "x")
    send = product(1, True, stacks, right)
    came = [shift(v, zl=1) for v in send]
    keep = product(1, False, stacks, right)
    bases = [swapped[1], base]
    parts = ladder_part(pair_amps, ladder_ints, pair_list)
    parts = lax.all_to_all(parts, "col", 0, 0)
    rows = ladder_sum(parts)

    stacks = ring(amps1, "y") + ring(amps2, "x")
    pieces = [
        (b.astype(F32) + (k + c.astype(F32))).astype(BF16) for b, k, c in zip(bases, keep, came)
    ]
    away = right_operand(pieces[0], -1)
    mine = right_operand(jnp.concatenate([pieces[1], rows], axis=0), 1)
    (send,) = product(2, True, stacks, away)
    came = shift(send, zl=1)
    (keep,) = product(2, False, stacks, mine)
    keep, *mine = lax.optimization_barrier((keep, *mine))
    ladder = ladder_end(mine)
    return (keep + came.astype(F32)).T, ladder


def solution(mesh):
    in_specs = (
        P("row", "col"),
        P("row", "col"),
        P("row", "col"),
        P("row", "col"),
        P("row", "col"),
        P(None, ("row", "col")),
        P(("row", "col"), None),
        P(),
    )
    out_specs = (P("row", "col"), P(None, "col"))
    return jax.shard_map(
        on_device, mesh=mesh, in_specs=in_specs, out_specs=out_specs, check_vma=False
    )
```

```python
import functools

import jax
import jax.numpy as jnp
from jax import lax
from jax.experimental import pallas as pl
from jax.experimental.pallas import tpu as pltpu
from jax.sharding import PartitionSpec as P


TILE = 64
F32, BF16 = jnp.float32, jnp.bfloat16
STEPS = (0, -1, 1, 2)


def shift(value, zh=0, core=0, y=0, x=0, zl=0):
    pairs = []
    for r in range(8):
        for c in range(32):
            to_r = ((r // 2 + zh) % 4) * 2 + (r + core) % 2
            to_c = ((c // 8 + y) % 4) * 8 + ((c // 2 + x) % 4) * 2 + (c + zl) % 2
            pairs.append((r * 32 + c, to_r * 32 + to_c))
    return lax.ppermute(value, ("row", "col"), pairs)


def ring(value, axis):
    return [value] + [shift(value, **{axis: -step}) for step in STEPS[1:]]


def place():
    r, c = lax.axis_index("row"), lax.axis_index("col")
    return r // 2, r % 2, c // 8, (c // 2) % 4, c % 2


def swap_middle(t):
    low = lax.broadcasted_iota(jnp.int32, t[0].shape, 1) < TILE
    r = [pltpu.roll(v, TILE, 1) if i in (1, 2, 3, 4) else v for i, v in enumerate(t)]
    return [
        t[0],
        jnp.where(low, t[1], r[3]),
        jnp.where(low, r[3], r[4]),
        jnp.where(low, r[1], r[2]),
        jnp.where(low, r[2], t[4]),
        t[5],
    ]


def prepare_kernel(v_ref, a_ref, b_ref, im_ref, am_ref, va1, va2, b_out, keep, send):
    low = lax.broadcasted_iota(jnp.int32, (TILE, 128), 1) < TILE
    zl = lax.axis_index("col") % 2
    for which, (ref, mask) in enumerate(((v_ref, im_ref), (a_ref, am_ref), (b_ref, im_ref))):
        for k in range(3):
            tiles = []
            for t in range(6):
                block = ref[k * 64 : k * 64 + 64, t * 128 : t * 128 + 128].astype(F32)
                m = jnp.where(low, mask[k, 2 * t], mask[k, 2 * t + 1]).astype(F32)
                tiles.append(block * m)
            tiles = [v.astype(BF16) for v in swap_middle(tiles)]
            rows = slice(k * 64, k * 64 + 64)
            halves = (tiles[0:3], tiles[3:6])
            if which == 0:
                halves = [
                    [jnp.where(zl == 0, p, q) for p, q in zip(*pair)]
                    for pair in ((halves[1], halves[0]), (halves[0], halves[1]))
                ]
            for at, half in enumerate(halves):
                if which == 2:
                    continue
                for t, v in enumerate(half):
                    lanes = slice(t * 128, t * 128 + 128)
                    if k == 0:
                        va1[2 * which + at, 0:64, lanes] = v
                    elif k == 1:
                        va1[2 * which + at, 64:96, lanes] = v[0:32]
                        va2[2 * which + at, 0:32, lanes] = v[32:64]
                    else:
                        va2[2 * which + at, 32:96, lanes] = v
            if which > 0:
                into = keep if which == 1 else b_out
                for t in range(3):
                    lanes = slice(t * 128, t * 128 + 128)
                    into[rows, lanes] = jnp.where(zl == 0, tiles[t], tiles[t + 3])
                    send[which - 1, rows, lanes] = jnp.where(zl == 0, tiles[t + 3], tiles[t])


VMEM = pl.BlockSpec(memory_space=pltpu.VMEM)
SMEM = pl.BlockSpec(memory_space=pltpu.SMEM)
ANY = pl.BlockSpec(memory_space=pl.ANY)


def prepare(vt, at, bt, int_mask, amp_mask):
    struct = jax.ShapeDtypeStruct
    return pl.pallas_call(
        prepare_kernel,
        name="prepare",
        compiler_params=pltpu.CompilerParams(vmem_limit_bytes=65600000),
        out_shape=(
            struct((4, 96, 384), BF16),
            struct((4, 96, 384), BF16),
            struct((192, 384), BF16),
            struct((192, 384), BF16),
            struct((2, 192, 384), BF16),
        ),
        in_specs=[VMEM, VMEM, VMEM, SMEM, SMEM],
        out_specs=(VMEM,) * 5,
        cost_estimate=pl.CostEstimate(flops=10**6, bytes_accessed=2 * 10**6, transcendentals=0),
    )(vt, at, bt, int_mask, amp_mask)


def join_kernel(a, b, out, sem):
    copies = []
    for i, ref in enumerate((a, b.at[0])):
        for lane in (0, 128, 256):
            lanes = pl.ds(lane, 128)
            into = out.at[pl.ds(192 * i, 192), lanes]
            copies.append(pltpu.make_async_copy(ref.at[:, lanes], into, sem))
    for copy in copies:
        copy.start()
    for copy in copies:
        copy.wait()


def join(a, b):
    return pl.pallas_call(
        join_kernel,
        name="join",
        out_shape=jax.ShapeDtypeStruct((384, 384), BF16),
        in_specs=[ANY] * 2,
        out_specs=VMEM,
        scratch_shapes=[pltpu.SemaphoreType.DMA],
        compiler_params=pltpu.CompilerParams(vmem_limit_bytes=4 << 20),
        cost_estimate=pl.CostEstimate(flops=1000, bytes_accessed=6 * 10**5, transcendentals=0),
    )(a, b)


def stack_kernel(a, b, c, d, ints, amps, sem):
    copies = []
    for i, ref in enumerate((a, b, c, d)):
        for part in range(4):
            into = (ints, amps)[part // 2].at[i, part % 2]
            for lane in (0, 128, 256):
                lanes = pl.ds(lane, 128)
                copies.append(
                    pltpu.make_async_copy(ref.at[part, :, lanes], into.at[:, lanes], sem)
                )
    for copy in copies:
        copy.start()
    for copy in copies:
        copy.wait()


def stack(blocks):
    struct = jax.ShapeDtypeStruct
    return pl.pallas_call(
        stack_kernel,
        name="stack",
        out_shape=(struct((4, 2, 96, 384), BF16), struct((4, 2, 96, 384), BF16)),
        in_specs=[ANY] * 4,
        out_specs=(VMEM,) * 2,
        scratch_shapes=[pltpu.SemaphoreType.DMA],
        compiler_params=pltpu.CompilerParams(vmem_limit_bytes=4 << 20),
        cost_estimate=pl.CostEstimate(flops=1000, bytes_accessed=2 * 10**6, transcendentals=0),
    )(*blocks)


def product_kernel(stage, sending, *refs):
    stacks, pieces, (*outs, w, g, total, w_sems, g_sems) = refs[:8], refs[8:16], refs[16:]
    zh, core, y, x, _ = place()
    count = g.shape[1]
    sides = ((0 if sending else 1),) if stage == 1 else (0, 1)

    for i, dz in enumerate(STEPS):
        for other in range(2):
            at_z, at_core = lax.rem(zh + dz + 4, 4), lax.rem(core + other, 2)
            pltpu.make_async_copy(
                pieces[other * 4 + i].at[pl.ds(0, count)],
                g.at[at_z, :, pl.ds(pl.multiple_of(at_core * 384, 128), 384)],
                g_sems.at[at_z],
            ).start()
    chunks = ((0, 128), (128, 256)) if stage == 1 else ((0, 384),)
    for down, dy in enumerate(STEPS):
        at_y = lax.rem(y + dy + 4, 4)
        for along, dx in enumerate(STEPS):
            row = (at_y * 4 + lax.rem(x + dx + 4, 4)) * 192
            for half in range(2):
                block = stacks[4 + along].at[down] if half else stacks[down].at[along]
                into = pl.ds(pl.multiple_of(row + half * 96, 32), 96)
                for at, side in enumerate(sides):
                    for lane, size in chunks:
                        pltpu.make_async_copy(
                            block.at[side, :, pl.ds(lane, size)],
                            w.at[into, pl.ds(at * 384 + lane, size)],
                            w_sems.at[at_y],
                        ).start()

    total[...] = jnp.zeros_like(total)

    @pl.loop(0, 4)
    def _(down):
        k = lax.rem(y + jnp.where(down < 2, 3 * down, down - 1), 4)
        part = pl.ds(pl.multiple_of(k * 768, 768), 768)
        pltpu.make_async_copy(w.at[part, :], w.at[part, :], w_sems.at[k]).wait()
        pltpu.make_async_copy(g.at[k], g.at[k], g_sems.at[k]).wait()
        total[...] += jnp.dot(g[k], w[part, :], preferred_element_type=F32)

    if stage == 2:
        (out,) = outs
        for k in range(3):
            part = slice(k * 64, k * 64 + 64)
            tiles = swap_middle([total[part, t * 128 : t * 128 + 128] for t in range(6)])
            for t, v in enumerate(tiles):
                out[part, t * 128 : t * 128 + 128] = v.astype(out.dtype)
    else:
        own, away = total[0:192], total[192:384]
        outs[0][...] = (own if sending else away).astype(outs[0].dtype)
        outs[1][...] = (away if sending else own).astype(outs[1].dtype)


def product(stage, sending, stacks, pieces):
    rows, width = (384, 384) if stage == 1 else (192, 768)
    return pl.pallas_call(
        functools.partial(product_kernel, stage, sending),
        out_shape=(jax.ShapeDtypeStruct((192, width), BF16 if sending else F32),) * (3 - stage),
        in_specs=[ANY] * 16,
        out_specs=(VMEM,) * (3 - stage),
        scratch_shapes=[
            pltpu.VMEM((3072, width), BF16),
            pltpu.VMEM((4, rows, 768), BF16),
            pltpu.VMEM((rows, width), F32),
            pltpu.SemaphoreType.DMA((4,)),
            pltpu.SemaphoreType.DMA((4,)),
        ],
        compiler_params=pltpu.CompilerParams(vmem_limit_bytes=16 << 20),
        cost_estimate=pl.CostEstimate(
            flops=384 * 768 * 3072, bytes_accessed=5 * 10**6, transcendentals=0
        ),
    )(*stacks, *pieces)


def right_operand(piece, via):
    before = shift(piece, zh=1)
    after = shift(piece, zh=-1)
    far = shift(after, zh=-1) if via < 0 else shift(before, zh=1)
    mine = [piece, before, after, far]
    return mine + [shift(v, core=1) for v in mine]


def ladder_kernel(pair_list, pair_amps, ladder_ints, out):
    row = lax.broadcasted_iota(jnp.int32, (16, 64), 0)
    column = lax.broadcasted_iota(jnp.int32, (16, 64), 1)
    wanted = jnp.zeros((16, 64), jnp.int32)
    for i in range(16):
        wanted = jnp.where(row == i, pair_list[i], wanted)
    selector = jnp.where(wanted == column, 1.0, 0.0).astype(BF16)
    chosen = jnp.dot(selector, pair_amps[...], preferred_element_type=F32).astype(BF16)
    sums = jnp.dot(chosen, ladder_ints[...], preferred_element_type=F32)
    for c in range(32):
        for j in range(4):
            out[c, :, j * 32 : j * 32 + 32] = sums[j * 4 : j * 4 + 4, c * 32 : c * 32 + 32]


def ladder_sum_kernel(parts, out):
    total = jnp.concatenate([jnp.sum(parts[...], axis=0), jnp.zeros((12, 128), F32)], axis=0)
    high = total.astype(BF16)
    out[:, 0:128] = high
    out[:, 128:256] = (total - high.astype(F32)).astype(BF16)
    out[:, 256:384] = jnp.zeros((16, 128), BF16)


def ladder_sum(parts):
    return pl.pallas_call(
        ladder_sum_kernel,
        name="ladder_sum",
        compiler_params=pltpu.CompilerParams(vmem_limit_bytes=1 << 20),
        out_shape=jax.ShapeDtypeStruct((16, 384), BF16),
        in_specs=[VMEM],
        out_specs=VMEM,
        cost_estimate=pl.CostEstimate(flops=20000, bytes_accessed=80000, transcendentals=0),
    )(parts)


def ladder_part(pair_amps, ladder_ints, pair_list):
    return pl.pallas_call(
        ladder_kernel,
        name="ladder",
        compiler_params=pltpu.CompilerParams(vmem_limit_bytes=6 << 20),
        out_shape=jax.ShapeDtypeStruct((32, 4, 128), F32),
        in_specs=[SMEM, VMEM, VMEM],
        out_specs=VMEM,
        cost_estimate=pl.CostEstimate(
            flops=25 * 10**6, bytes_accessed=2 * 10**6, transcendentals=0
        ),
    )(pair_list, pair_amps, ladder_ints)


def ladder_end_kernel(*refs):
    pieces, (out, rows, sem) = refs[:8], refs[8:]
    copies = []
    for i, ref in enumerate(pieces):
        copies.append(pltpu.make_async_copy(ref.at[pl.ds(192, 16)], rows.at[i], sem))
    for copy in copies:
        copy.start()
    for copy in copies:
        copy.wait()
    total = rows[0].astype(F32)
    for i in range(1, 8):
        total += rows[i].astype(F32)
    total = total[0:4, 0:128] + total[0:4, 128:256]
    for j in range(4):
        out[j * 4 : j * 4 + 4, :] = total[:, j * 32 : j * 32 + 32]


def ladder_end(pieces):
    return pl.pallas_call(
        ladder_end_kernel,
        name="ladder_end",
        out_shape=jax.ShapeDtypeStruct((16, 32), F32),
        in_specs=[ANY] * 8,
        out_specs=VMEM,
        scratch_shapes=[pltpu.VMEM((8, 16, 384), BF16), pltpu.SemaphoreType.DMA],
        compiler_params=pltpu.CompilerParams(vmem_limit_bytes=1 << 20),
        cost_estimate=pl.CostEstimate(flops=20000, bytes_accessed=100000, transcendentals=0),
    )(*pieces)


def on_device(
    tile_amps, cycle_ints, base_ints, amp_mask, int_mask, pair_amps, ladder_ints, pair_list
):
    va1, va2, base, keep, send = prepare(
        cycle_ints.T, tile_amps.T, base_ints.T, int_mask.T, amp_mask.T
    )
    swapped = shift(send, zl=1)
    x_blocks, y_blocks = ring(va1, "x"), ring(va2, "y")
    right = right_operand(join(keep, swapped), -1)
    ints1, amps1 = stack(x_blocks)
    ints2, amps2 = stack(y_blocks)
    stacks = ring(ints1, "y") + ring(ints2, "x")
    send = product(1, True, stacks, right)
    came = [shift(v, zl=1) for v in send]
    keep = product(1, False, stacks, right)
    bases = [swapped[1], base]
    parts = ladder_part(pair_amps, ladder_ints, pair_list)
    parts = lax.all_to_all(parts, "col", 0, 0)
    rows = ladder_sum(parts)

    stacks = ring(amps1, "y") + ring(amps2, "x")
    pieces = [
        (b.astype(F32) + (k + c.astype(F32))).astype(BF16) for b, k, c in zip(bases, keep, came)
    ]
    away = right_operand(pieces[0], -1)
    mine = right_operand(jnp.concatenate([pieces[1], rows], axis=0), 1)
    (send,) = product(2, True, stacks, away)
    came = shift(send, zl=1)
    (keep,) = product(2, False, stacks, mine)
    keep, *mine = lax.optimization_barrier((keep, *mine))
    ladder = ladder_end(mine)
    return (keep + came.astype(F32)).T, ladder


def solution(mesh):
    in_specs = (
        P("row", "col"),
        P("row", "col"),
        P("row", "col"),
        P("row", "col"),
        P("row", "col"),
        P(None, ("row", "col")),
        P(("row", "col"), None),
        P(),
    )
    out_specs = (P("row", "col"), P(None, "col"))
    return jax.shard_map(
        on_device, mesh=mesh, in_specs=in_specs, out_specs=out_specs, check_vma=False
    )
```
